1024 devices in a mesh: seq: 4 (over x), exp: 32 (over z, core), head: 8 (over y).
Axes of the slice: x: 4, y: 8, z: 16, core: 2. Of those that a mesh axis runs over, the one named last changes fastest.
Arguments:
- out_grad: bfloat16 [12288, 2048], P(('exp', 'head')), may hold values from -6 to 6
- layer_input: bfloat16 [12288, 2048], P(('exp', 'head')), may hold values from -6 to 6
- norm_gain: float32 [2048], replicated, may hold values from 0.5 to 1.5
- routes: int32 [12288, 8], P(('exp', 'head')), may hold values from 0 to 63, all different within a row; in each aligned block of 48 rows (0 to 47, 48 to 95, ...) at most 8 rows name the same one
- gates: float32 [12288, 8], P(('exp', 'head')), may hold values from 0.02 to 0.3
- gate_pre: bfloat16 [8, 64, 32, 8, 768], P('head', 'exp', None, None, 'seq'), may hold values from -6 to 6
- up_pre: bfloat16 [8, 64, 32, 8, 768], P('head', 'exp', None, None, 'seq'), may hold values from -6 to 6
- w_gate: bfloat16 [64, 2048, 768], P('exp', None, 'seq'), may hold values from -0.125 to 0.125
- w_up: bfloat16 [64, 2048, 768], P('exp', None, 'seq'), may hold values from -0.125 to 0.125
- w_down: bfloat16 [64, 768, 2048], P('exp', 'seq'), may hold values from -0.21875 to 0.21875
- w_out: bfloat16 [4096, 2048], P('head'), may hold values from -0.09375 to 0.09375
Outputs:
- resid_grad: float32 [4, 3072, 2048], P('seq', ('exp', 'head'))
- head_grad: bfloat16 [4, 3072, 4096], P('seq', 'exp', 'head')
The draws below stay inside these ranges and needn't reach their ends.
Inputs may be any that keep to these rules, and one draw needn't show every extreme that they name: `routes`: each row names 8 different experts. In each aligned block of 48 rows (the tokens of one device) no expert is named by more than 8 rows, a bound that some block reaches.
All inputs are finite; a program needn't handle non-finite values.
Results may differ from the reference program's by a relative error of at most 0.0095.
Values may be sent and summed in bfloat16 or wider, within the bound.
No kernel may reach another device: no remote copies, remote signals or barrier semaphores. Data moves between devices by JAX's collectives and lax.ppermute only.
A program may use at most 32 MiB of HBM per device.

```python
import math
import jax
import jax.numpy as jnp
import numpy as np
from jax import lax

D = 2048
FF = 768
TOPK = 8
TOK_DEV = 48
EXPERTS = 64
CAP = 8
ATTN = 4096
SEQ_GROUPS = 4
EXP_GROUPS = 32
HEAD_GROUPS = 8
TOKENS = 12288


def levels(key, extent, cuts, low, top_value):
    gain = 1.0
    for dim, parts in cuts:
        heights = jax.random.uniform(jax.random.fold_in(jax.random.fold_in(key, 6), dim), (parts,), jnp.float32, low / len(cuts), top_value / len(cuts))
        gain = gain * jnp.repeat(jnp.exp(heights), extent[dim] // parts).reshape((-1,) + (1,) * (len(extent) - 1 - dim))
    return gain


def shared_out(rng, own, number, rows, number_of, top, most, slope):
    order = jax.random.permutation(rng, number_of)
    heavy_load, ordinary = shares(number_of, rows * top, most, slope, True), shares(number_of, rows * top, most, slope, False)
    places = jnp.arange(number_of)

    def named(lengths, turn):
        used = int((lengths > 0).sum())
        fixed = max(1, used // 4)
        passed = fixed + (places - fixed + turn * (used - fixed)) % max(1, number_of - fixed)
        return jnp.zeros((number_of,), jnp.int32).at[order[jnp.where(places < fixed, places, passed)]].set(jnp.asarray(lengths, jnp.int32))

    lengths = jnp.where(number % 4 == 0, named(heavy_load, number // 4), named(ordinary, number - number // 4 - 1))
    mixed = jax.random.permutation(jax.random.fold_in(own, 3), number_of)
    giver, sink = mixed[0:number_of // 2 * 2:2], mixed[1:number_of // 2 * 2:2]
    room = jnp.minimum(lengths[giver] - 1, most - lengths[sink]) // 2
    room = jnp.where((giver == order[0]) | (sink == order[0]) | (lengths[sink] == 0), 0, jnp.maximum(room, 0))
    passed = jax.random.randint(jax.random.fold_in(own, 4), (number_of // 2,), 0, 1 << 20) % (room + 1)
    lengths = lengths.at[giver].add(-passed).at[sink].add(passed)
    items = jnp.searchsorted(jnp.cumsum(lengths), jnp.arange(rows * top), side="right").astype(jnp.int32)
    table = items.reshape(top, rows).T
    table = table[jax.random.permutation(jax.random.fold_in(own, 1), rows)]
    turn = jax.random.randint(jax.random.fold_in(own, 2), (rows, 1), 0, top)
    return jnp.take_along_axis(table, (jnp.arange(top)[None, :] + turn) % top, axis=1)


def shares(amount, total, bound, skew, full):
    loads = [(1 << 20) // math.isqrt(grade ** skew) + 1 for grade in range(1, amount + 1)]
    largest = bound if full else min(bound, max(-(-total // amount), total * loads[0] // sum(loads)))
    least = 1 if total - largest >= amount - 1 else 0
    counts, surplus = [largest] + [least] * (amount - 1), total - largest - least * (amount - 1)
    while surplus > 0:
        movable = [i for i in range(1, amount) if counts[i] < largest] or [i for i in range(1, amount) if counts[i] < bound]
        mass, left = sum([loads[i] for i in movable]), surplus
        for i in movable:
            extra = min(bound - counts[i], max(1, left * loads[i] // mass), surplus)
            counts[i] = counts[i] + extra
            surplus = surplus - extra
    return np.array(counts)


def normal_values(rng, extent, deviation, reach, split=(), kind=jnp.bfloat16):
    result = jax.random.normal(rng, extent, jnp.float32) * deviation
    if len(split) > 0:
        result = levels(rng, extent, split, -0.22, 0.18) * result
    return jnp.clip(result, min=-reach, max=reach).astype(kind)


def setup_inputs(seed: int = 0) -> dict:
    key_of = jax.random.split(jax.random.key(seed), 12)
    out_grad = normal_values(key_of[0], (TOKENS, D), 1.0, 6.0, ((0, 256),))
    layer_input = normal_values(key_of[1], (TOKENS, D), 1.0, 6.0, ((0, 256),))
    norm_gain = jnp.clip(1.0 + 0.1 * jax.random.normal(key_of[2], (D,), jnp.float32), 0.5, 1.5)
    routes_keys = jax.random.split(jax.random.fold_in(key_of[3], 1), TOKENS // TOK_DEV)
    routes_turns = jax.random.permutation(jax.random.fold_in(key_of[3], 3), TOKENS // TOK_DEV)
    routes = jax.vmap(lambda own, number: shared_out(jax.random.fold_in(key_of[3], 2), own, number, TOK_DEV, EXPERTS, TOPK, CAP, 2))(routes_keys, routes_turns).reshape((TOKENS, TOPK))
    gates = jnp.clip(0.02 + 0.28 * jax.random.uniform(key_of[4], (TOKENS, TOPK), jnp.float32) ** levels(key_of[4], (TOKENS, TOPK), ((0, 256),), -0.2, 0.2), 0.02, 0.3)
    gate_pre = normal_values(key_of[5], (HEAD_GROUPS, EXPERTS, EXP_GROUPS, CAP, FF), 1.0, 6.0, ((0, 8), (1, 32), (4, 4)))
    up_pre = normal_values(key_of[6], (HEAD_GROUPS, EXPERTS, EXP_GROUPS, CAP, FF), 1.0, 6.0, ((0, 8), (1, 32), (4, 4)))
    w_gate = normal_values(key_of[7], (EXPERTS, D, FF), D ** -0.5, 0.125, ((0, 32), (2, 4)))
    w_up = normal_values(key_of[8], (EXPERTS, D, FF), D ** -0.5, 0.125, ((0, 32), (2, 4)))
    w_down = normal_values(key_of[9], (EXPERTS, FF, D), FF ** -0.5, 0.21875, ((0, 32), (1, 4)))
    w_out = normal_values(key_of[10], (ATTN, D), ATTN ** -0.5, 0.09375, ((0, 8),))
    return {"out_grad": out_grad, "layer_input": layer_input, "norm_gain": norm_gain, "routes": routes, "gates": gates, "gate_pre": gate_pre, "up_pre": up_pre, "w_gate": w_gate, "w_up": w_up, "w_down": w_down, "w_out": w_out}


def reference(out_grad, layer_input, norm_gain, routes, gates, gate_pre, up_pre, w_gate, w_up, w_down, w_out):
    block_count = HEAD_GROUPS * EXP_GROUPS
    expert_ids = jnp.arange(EXPERTS, dtype=jnp.int32)
    block_routes = routes.reshape(block_count, TOK_DEV * TOPK)
    onehot = (block_routes[:, :, None] == expert_ids[None, None, :]).astype(jnp.int32)
    position = lax.optimization_barrier(jnp.sum((jnp.cumsum(onehot, axis=1) - 1) * onehot, axis=2)).reshape(TOKENS, TOPK)
    block_id = jnp.arange(TOKENS, dtype=jnp.int32) // TOK_DEV
    source_exp = block_id // HEAD_GROUPS
    source_head = block_id % HEAD_GROUPS
    buffer_row = ((source_head * EXP_GROUPS + source_exp)[:, None] * CAP + position).astype(jnp.int32)
    grad_wide = out_grad.astype(jnp.float32)
    slot_total = HEAD_GROUPS * EXP_GROUPS * CAP
    quarter_ff = FF // SEQ_GROUPS

    def one_expert(carry, expert):
        chosen = routes == expert
        valid = jnp.any(chosen, axis=1)
        row_index = lax.optimization_barrier(jnp.sum(jnp.where(chosen, buffer_row, 0), axis=1)).astype(jnp.int32)
        weight = lax.optimization_barrier(jnp.sum(jnp.where(chosen, gates, 0.0), axis=1))
        scaled = (weight[:, None] * grad_wide).astype(jnp.bfloat16)
        target = jnp.where(valid, row_index, slot_total).astype(jnp.int32)
        slot_rows = jnp.zeros((slot_total, D), jnp.bfloat16).at[target].set(scaled, mode='drop')
        gate_act = lax.dynamic_index_in_dim(gate_pre, expert, 1, keepdims=False).reshape(slot_total, FF).astype(jnp.float32)
        up_act = lax.dynamic_index_in_dim(up_pre, expert, 1, keepdims=False).reshape(slot_total, FF).astype(jnp.float32)
        down_here = lax.dynamic_index_in_dim(w_down, expert, 0, keepdims=False)
        gate_here = lax.dynamic_index_in_dim(w_gate, expert, 0, keepdims=False)
        up_here = lax.dynamic_index_in_dim(w_up, expert, 0, keepdims=False)
        d_hidden = jnp.dot(slot_rows, down_here.T, preferred_element_type=jnp.float32)
        sigmoid_gate = jax.nn.sigmoid(gate_act)
        silu_gate = gate_act * sigmoid_gate
        silu_slope = sigmoid_gate * (1.0 + gate_act * (1.0 - sigmoid_gate))
        d_gate = (d_hidden * up_act * silu_slope).astype(jnp.bfloat16)
        d_up = (d_hidden * silu_gate).astype(jnp.bfloat16)
        gate_part = d_gate.astype(jnp.float32).reshape(slot_total, SEQ_GROUPS, quarter_ff)
        up_part = d_up.astype(jnp.float32).reshape(slot_total, SEQ_GROUPS, quarter_ff)
        gate_cols = gate_here.astype(jnp.float32).reshape(D, SEQ_GROUPS, quarter_ff)
        up_cols = up_here.astype(jnp.float32).reshape(D, SEQ_GROUPS, quarter_ff)
        quarters = jnp.einsum('rqf,dqf->qrd', gate_part, gate_cols) + jnp.einsum('rqf,dqf->qrd', up_part, up_cols)
        rounded = lax.optimization_barrier(quarters.astype(jnp.bfloat16))
        slot_part = lax.optimization_barrier(jnp.sum(rounded.astype(jnp.float32), axis=0))
        picked = slot_part[row_index]
        carry = carry + jnp.where(valid[:, None], picked, 0.0)
        return (carry, None)
    moe_grad, unused = lax.scan(one_expert, jnp.zeros((TOKENS, D), jnp.float32), expert_ids)
    inputs = layer_input.astype(jnp.float32)
    inv_rms = lax.rsqrt(lax.optimization_barrier(jnp.mean(inputs * inputs, axis=1, keepdims=True)) + 1e-06)
    normed = inputs * inv_rms
    scaled_grad = moe_grad * norm_gain[None, :]
    full_grad = grad_wide + inv_rms * (scaled_grad - normed * lax.optimization_barrier(jnp.mean(scaled_grad * normed, axis=1, keepdims=True)))
    head_full = jnp.dot(full_grad.astype(jnp.bfloat16), w_out.T, preferred_element_type=jnp.float32).astype(jnp.bfloat16)

    def arrange(values):
        shaped = values.reshape(block_count, SEQ_GROUPS, TOK_DEV // SEQ_GROUPS, values.shape[1])
        return shaped.transpose(1, 0, 2, 3).reshape(SEQ_GROUPS, TOKENS // SEQ_GROUPS, values.shape[1])
    return (arrange(full_grad), arrange(head_full))
```

```python
import functools

import jax
import jax.numpy as jnp
from jax import lax
from jax.experimental import pallas as pl
from jax.experimental.pallas import tpu as pltpu
from jax.sharding import PartitionSpec as P

BF = jnp.bfloat16
F32 = jnp.float32
I32 = jnp.int32
VM = pl.BlockSpec(memory_space=pltpu.VMEM)
SM = pl.BlockSpec(memory_space=pltpu.SMEM)
PAD = 16
LANES = 128
GRANT = 24 << 20


def iota(shape, dim):
    return lax.broadcasted_iota(I32, shape, dim)


def one_hot(where):
    return jnp.where(where, 1.0, 0.0).astype(BF)


def dot(a, b):
    return jnp.dot(a, b, preferred_element_type=F32)


def dot_t(a, b):
    return lax.dot_general(a, b, (((1,), (1,)), ((), ())), preferred_element_type=F32)


def dispatch_kernel(capacity, quarter_ref, routes_ref, gates_ref, grad_ref, slots_ref, pick_ref):
    top, tok_count = routes_ref.shape
    rows, piece = slots_ref.shape
    start = pl.multiple_of(quarter_ref[0] * piece, piece)
    cols = grad_ref[:, pl.ds(start, piece)]
    square = (tok_count, tok_count)
    earlier = one_hot(iota(square, 0) < iota(square, 1))
    row = iota((rows, tok_count), 0)
    expert = row // capacity
    named = jnp.zeros((rows, tok_count), F32)
    gate = jnp.zeros((rows, tok_count), F32)
    for k in range(top):
        hit = routes_ref[k : k + 1, :] == expert
        named = jnp.where(hit, 1.0, named)
        gate = jnp.where(hit, gates_ref[k : k + 1, :], gate)
    count = dot(named.astype(BF), earlier)
    here = (named > 0.0) & (count == (row % capacity).astype(F32))
    weight = jnp.sum(jnp.where(here, gate, 0.0), axis=1, keepdims=True)
    pick = one_hot(here)
    pick_ref[...] = pick
    slots_ref[...] = (dot(pick, cols) * weight).astype(BF)


def hidden_kernel(quarter_ref, rows_ref, *refs):
    downs, out_ref = refs[:-1], refs[-1]
    groups, block, piece = rows_ref.shape
    experts_here, hidden, _ = downs[0].shape
    capacity = block // experts_here
    quarters = len(downs)
    wide = rows_ref[...].astype(F32)
    for j in range(experts_here):
        mine = wide[:, j * capacity : (j + 1) * capacity, :]
        mine = mine.reshape(groups * capacity, piece).astype(BF)
        for d in range(quarters):
            target = lax.rem(quarter_ref[0] + quarters - d, quarters)
            value = dot_t(downs[d][j], mine)
            out_ref[target, j * hidden : (j + 1) * hidden, :] = value.astype(BF)


def expert_kernel(parts_ref, gate_ref, up_ref, wg_ref, wu_ref, out_ref):
    quarters, groups, block, piece = out_ref.shape
    experts_here, hidden, _ = wg_ref.shape
    capacity = block // experts_here
    rows = groups * capacity
    grads = []
    for j in range(experts_here):
        band = slice(j * hidden, (j + 1) * hidden)
        total = parts_ref[0, band, :].astype(F32)
        for c in range(1, quarters):
            total = total + parts_ref[c, band, :].astype(F32)
        d_hidden = total.T
        act = gate_ref[j].astype(F32)
        up = up_ref[j].astype(F32)
        sig = jax.nn.sigmoid(act)
        d_gate = (d_hidden * up * (sig * (1.0 + act * (1.0 - sig)))).astype(BF)
        d_up = (d_hidden * (act * sig)).astype(BF)
        grads.append((d_gate, d_up))
    for c in range(quarters):
        cols = slice(c * piece, (c + 1) * piece)
        values = []
        for j in range(experts_here):
            value = dot(grads[j][0], wg_ref[j, :, cols]) + dot(grads[j][1], wu_ref[j, :, cols])
            values.append(value.reshape(groups, capacity, piece))
        out_ref[c] = jnp.concatenate(values, axis=1).astype(BF)


def sum_kernel(parts_ref, out_ref):
    total = parts_ref[0].astype(F32)
    for c in range(1, parts_ref.shape[0]):
        total = total + parts_ref[c].astype(F32)
    out_ref[...] = total.astype(BF)


def combine_kernel(pick_ref, back_ref, out_ref):
    quarters, heads, packed, lanes = out_ref.shape
    tok_count = pick_ref.shape[1]
    part = tok_count // quarters
    tiles = packed // part
    total = lax.dot_general(
        pick_ref[...], back_ref[...], (((0,), (0,)), ((), ())), preferred_element_type=F32
    ).astype(BF)
    to = iota((packed, tok_count), 0)
    token = iota((packed, tok_count), 1)
    for c in range(quarters):
        value = jnp.zeros((packed, lanes), F32)
        for n in range(tiles):
            move = one_hot((to // part == n) & (c * part + to % part == token))
            value = value + dot(move, total[:, n * lanes : (n + 1) * lanes])
        value = value.astype(BF)
        for h in range(heads):
            out_ref[c, h] = value


def offset(index, heads):
    turned = jnp.zeros_like(index)
    step = 1
    while step < heads:
        turned = turned * 2 + index // step % 2
        step *= 2
    return turned


def finish_kernel(head_ref, moe_ref, pairs_ref, gain_ref, w_ref, resid_ref, grad_ref, moe):
    quarters, heads, packed, lanes = moe_ref.shape
    part, width = resid_ref.shape
    tiles = packed // part
    piece = tiles * lanes
    rows = heads * PAD
    me = head_ref[0]
    row = iota((rows, heads * packed), 0)
    source = offset(row // PAD, heads) ^ me
    item = iota((rows, heads * packed), 1)
    for n in range(tiles):
        want = source * packed + n * part + row % PAD
        move = one_hot((want == item) & (row % PAD < part))
        for c in range(quarters):
            block = moe_ref[c].reshape(heads * packed, lanes)
            start = c * piece + n * lanes
            moe[:, start : start + lanes] = dot(move, block)
    row = iota((rows, heads * 2 * part), 0)
    item = iota((rows, heads * 2 * part), 1)
    first = (row // PAD) * (2 * part) + row % PAD
    real = row % PAD < part
    pairs = pairs_ref[...]
    x = dot(one_hot((item == first) & real), pairs)
    inv_rms = lax.rsqrt(jnp.sum(x * x, axis=1, keepdims=True) / width + 1e-06)
    normed = x * inv_rms
    scaled = moe[...] * gain_ref[...]
    mean = jnp.sum(scaled * normed, axis=1, keepdims=True) / width
    out_rows = dot(one_hot((item == first + part) & real), pairs)
    full = out_rows + inv_rms * (scaled - normed * mean)
    resid_ref[...] = full[:part]
    product = dot_t(full.astype(BF), w_ref[...]).astype(BF)
    want = iota((heads * part, rows), 0)
    have = iota((heads * part, rows), 1)
    keep = one_hot(offset((want // part) ^ me, heads) * PAD + want % part == have)
    grad_ref[...] = dot(keep, product).astype(BF)


def call(kernel, out_shape, specs, flops, moved, scratch=()):
    return pl.pallas_call(
        kernel,
        out_shape=out_shape,
        in_specs=specs,
        out_specs=jax.tree.map(lambda _: VM, out_shape),
        scratch_shapes=scratch,
        cost_estimate=pl.CostEstimate(flops=flops, bytes_accessed=moved, transcendentals=0),
        compiler_params=pltpu.CompilerParams(vmem_limit_bytes=GRANT),
    )


def exchange(blocks, axis):
    return lax.all_to_all(blocks, axis, split_axis=0, concat_axis=0, tiled=True)


def shards(
    out_grad, layer_input, norm_gain, routes, gates, gate_pre, up_pre, w_gate, w_up, w_down, w_out
):
    experts_here = w_gate.shape[0]
    exp_groups = lax.axis_size("exp")
    quarters = lax.axis_size("seq")
    heads = lax.axis_size("head")
    capacity = gate_pre.shape[3]
    hidden = gate_pre.shape[4]
    tok_count, width = out_grad.shape
    piece = width // quarters
    part = tok_count // quarters
    block = experts_here * capacity
    rows = exp_groups * block
    attn = w_out.shape[0]
    packed = part * piece // LANES
    sds = jax.ShapeDtypeStruct
    quarter = lax.axis_index("seq").astype(I32).reshape(1)
    head = lax.axis_index("head").astype(I32).reshape(1)

    slots, pick = call(
        functools.partial(dispatch_kernel, capacity),
        [sds((rows, piece), BF), sds((rows, tok_count), BF)],
        [SM, VM, VM, VM],
        2 * rows * tok_count * piece,
        1 << 20,
    )(quarter, routes.T, gates.T, out_grad)

    received = exchange(slots.reshape(exp_groups, block, piece), "exp")

    downs = []
    for d in range(quarters):
        start = lax.rem(quarter[0] + d, quarters) * piece
        own = lax.dynamic_slice_in_dim(w_down, start, piece, 2)
        ring = [(i, (i + d) % quarters) for i in range(quarters)]
        downs.append(lax.ppermute(own, "seq", ring) if d else own)

    def own_rows(values):
        return lax.dynamic_slice_in_dim(values, quarter[0] * part, part, 0)

    def doubled(values, step):
        other = lax.ppermute(values, "head", [(i, i ^ step) for i in range(heads)])
        return jnp.concatenate([values, other], axis=0)

    pairs = jnp.concatenate([own_rows(layer_input), own_rows(out_grad)], axis=0)
    pairs = doubled(pairs, heads // 2)
    downs, pairs = lax.optimization_barrier((downs, pairs))

    partial_hidden = call(
        hidden_kernel,
        sds((quarters, experts_here * hidden, exp_groups * capacity), BF),
        [SM] + [VM] * (1 + quarters),
        2 * rows * width * hidden,
        3 << 20,
    )(quarter, received, *downs)
    summands = exchange(partial_hidden, "seq")
    parts = call(
        expert_kernel,
        sds((quarters, exp_groups, block, piece), BF),
        [VM] * 5,
        4 * rows * hidden * width,
        6 << 20,
    )(
        summands,
        gate_pre.reshape(experts_here, exp_groups * capacity, hidden),
        up_pre.reshape(experts_here, exp_groups * capacity, hidden),
        jnp.swapaxes(w_gate, 1, 2),
        jnp.swapaxes(w_up, 1, 2),
    )
    mine = exchange(parts, "seq")
    if heads > 2:
        pairs = doubled(pairs, heads // 4)
    mine, pairs = lax.optimization_barrier((mine, pairs))
    summed = call(
        sum_kernel, sds((exp_groups, block, piece), BF), [VM], 4 * rows * piece, 3 << 20
    )(mine)
    back = exchange(summed, "exp")
    step = heads // 8
    while step > 0:
        pairs = doubled(pairs, step)
        step //= 2
    back, pairs = lax.optimization_barrier((back, pairs))
    combined = call(
        combine_kernel,
        sds((quarters, heads, packed, LANES), BF),
        [VM] * 2,
        2 * rows * tok_count * piece,
        1 << 20,
    )(pick, back.reshape(rows, piece))
    got = exchange(combined.reshape(quarters * heads, packed, LANES), ("seq", "head"))
    resid, head_grad = call(
        finish_kernel,
        [sds((part, width), F32), sds((heads * part, attn), BF)],
        [SM] + [VM] * 4,
        2 * heads * PAD * width * attn,
        4 << 20,
        [pltpu.VMEM((heads * PAD, width), F32)],
    )(head, got.reshape(quarters, heads, packed, LANES), pairs, norm_gain[None, :], w_out)
    return resid[None], head_grad[None]


def solution(mesh):
    placed = (
        P(("exp", "head"), None),
        P(("exp", "head"), None),
        P(),
        P(("exp", "head"), None),
        P(("exp", "head"), None),
        P("head", "exp", None, None, "seq"),
        P("head", "exp", None, None, "seq"),
        P("exp", None, "seq"),
        P("exp", None, "seq"),
        P("exp", "seq", None),
        P("head", None),
    )
    return jax.shard_map(
        shards,
        mesh=mesh,
        in_specs=placed,
        out_specs=(P("seq", ("exp", "head"), None), P("seq", "exp", "head")),
        check_vma=False,
    )
```

```python
import functools

import jax
import jax.numpy as jnp
from jax import lax
from jax.experimental import pallas as pl
from jax.experimental.pallas import tpu as pltpu
from jax.sharding import PartitionSpec as P

BF = jnp.bfloat16
F32 = jnp.float32
I32 = jnp.int32
VM = pl.BlockSpec(memory_space=pltpu.VMEM)
SM = pl.BlockSpec(memory_space=pltpu.SMEM)
HB = pl.BlockSpec(memory_space=pltpu.HBM)
DMA = pltpu.SemaphoreType.DMA
PAD = 16
LANES = 128
GRANT = 12 << 20


def iota(shape, dim):
    return lax.broadcasted_iota(I32, shape, dim)


def one_hot(where):
    return jnp.where(where, 1.0, 0.0).astype(BF)


def dot(a, b):
    return jnp.dot(a, b, preferred_element_type=F32)


def dot_t(a, b):
    return lax.dot_general(a, b, (((1,), (1,)), ((), ())), preferred_element_type=F32)


def slot_hits(routes, capacity, rows):
    top, tok_count = routes.shape
    square = (tok_count, tok_count)
    earlier = one_hot(iota(square, 0) < iota(square, 1))
    row = iota((rows, tok_count), 0)
    hits = [routes[k : k + 1, :] == row // capacity for k in range(top)]
    named = jnp.zeros((rows, tok_count), F32)
    for hit in hits:
        named = jnp.where(hit, 1.0, named)
    count = dot(named.astype(BF), earlier)
    here = (named > 0.0) & (count == (row % capacity).astype(F32))
    return hits, here


def dispatch_kernel(
    capacity, quarter_ref, routes_hbm, gates_hbm, grad_hbm, slots_ref, routes_ref, gates_ref, cols_ref, sems
):
    rows, piece = slots_ref.shape
    start = pl.multiple_of(quarter_ref[0] * piece, piece)
    copies = [
        pltpu.make_async_copy(routes_hbm, routes_ref, sems.at[0]),
        pltpu.make_async_copy(gates_hbm, gates_ref, sems.at[1]),
        pltpu.make_async_copy(grad_hbm.at[:, pl.ds(start, piece)], cols_ref, sems.at[2]),
    ]
    for copy in copies:
        copy.start()
    copies[0].wait()
    hits, here = slot_hits(routes_ref[...], capacity, rows)
    copies[1].wait()
    gate = jnp.zeros(here.shape, F32)
    for k, hit in enumerate(hits):
        gate = jnp.where(hit, gates_ref[k : k + 1, :], gate)
    weight = jnp.sum(jnp.where(here, gate, 0.0), axis=1, keepdims=True)
    copies[2].wait()
    slots_ref[...] = (dot(one_hot(here), cols_ref[...]) * weight).astype(BF)


def pick_kernel(capacity, routes_ref, pick_ref):
    tok_count, rows = pick_ref.shape
    _, here = slot_hits(routes_ref[...], capacity, rows)
    square = (tok_count, tok_count)
    pick_ref[...] = dot_t(one_hot(iota(square, 0) == iota(square, 1)), one_hot(here)).astype(BF)


def hidden_kernel(quarter_ref, rows_ref, *refs):
    downs, out_ref = refs[:-1], refs[-1]
    groups, block, piece = rows_ref.shape
    experts_here, hidden, _ = downs[0].shape
    capacity = block // experts_here
    quarters = len(downs)
    wide = rows_ref[...].astype(F32)
    for j in range(experts_here):
        mine = wide[:, j * capacity : (j + 1) * capacity, :]
        mine = mine.reshape(groups * capacity, piece).astype(BF)
        for d in range(quarters):
            target = lax.rem(quarter_ref[0] + quarters - d, quarters)
            value = dot_t(downs[d][j], mine)
            out_ref[target, j * hidden : (j + 1) * hidden, :] = value.astype(BF)


def expert_kernel(parts_ref, gate_ref, up_ref, wg_ref, wu_ref, out_hbm, out, sems):
    quarters, groups, block, piece = out.shape
    experts_here, hidden, _ = wg_ref.shape
    capacity = block // experts_here
    grads = []
    for j in range(experts_here):
        band = slice(j * hidden, (j + 1) * hidden)
        total = parts_ref[0, band, :].astype(F32)
        for c in range(1, quarters):
            total = total + parts_ref[c, band, :].astype(F32)
        d_hidden = total.T
        act = gate_ref[j].astype(F32)
        up = up_ref[j].astype(F32)
        sig = jax.nn.sigmoid(act)
        d_gate = (d_hidden * up * (sig * (1.0 + act * (1.0 - sig)))).astype(BF)
        d_up = (d_hidden * (act * sig)).astype(BF)
        grads.append((d_gate, d_up))
    copies = []
    for c in range(quarters):
        cols = slice(c * piece, (c + 1) * piece)
        values = []
        for j in range(experts_here):
            value = dot(grads[j][0], wg_ref[j, :, cols]) + dot(grads[j][1], wu_ref[j, :, cols])
            values.append(value.reshape(groups, capacity, piece))
        out[c] = jnp.concatenate(values, axis=1).astype(BF)
        copies.append(pltpu.make_async_copy(out.at[c], out_hbm.at[c], sems.at[c]))
        copies[-1].start()
    for copy in copies:
        copy.wait()


def sum_kernel(parts_ref, out_ref):
    total = parts_ref[0].astype(F32)
    for c in range(1, parts_ref.shape[0]):
        total = total + parts_ref[c].astype(F32)
    out_ref[...] = total.astype(BF)


def combine_kernel(pick_ref, back_ref, out_ref):
    quarters, heads, packed, lanes = out_ref.shape
    tok_count = pick_ref.shape[0]
    part = tok_count // quarters
    tiles = packed // part
    total = dot(pick_ref[...], back_ref[...]).astype(BF)
    to = iota((packed, tok_count), 0)
    token = iota((packed, tok_count), 1)
    for c in range(quarters):
        value = jnp.zeros((packed, lanes), F32)
        for n in range(tiles):
            move = one_hot((to // part == n) & (c * part + to % part == token))
            value = value + dot(move, total[:, n * lanes : (n + 1) * lanes])
        value = value.astype(BF)
        for h in range(heads):
            out_ref[c, h] = value


def offset(index, heads):
    turned = jnp.zeros_like(index)
    step = 1
    while step < heads:
        turned = turned * 2 + index // step % 2
        step *= 2
    return turned


def finish_kernel(head_ref, moe_ref, pairs_ref, gain_ref, w_ref, resid_ref, grad_ref, moe):
    quarters, heads, packed, lanes = moe_ref.shape
    part, _, width = resid_ref.shape
    tiles = packed // part
    piece = tiles * lanes
    rows = heads * PAD
    me = head_ref[0]
    row = iota((rows, heads * packed), 0)
    source = offset(row // PAD, heads) ^ me
    item = iota((rows, heads * packed), 1)
    for n in range(tiles):
        want = source * packed + n * part + row % PAD
        move = one_hot((want == item) & (row % PAD < part))
        for c in range(quarters):
            block = moe_ref[c].reshape(heads * packed, lanes)
            start = c * piece + n * lanes
            moe[:, start : start + lanes] = dot(move, block)
    row = iota((rows, heads * 2 * part), 0)
    item = iota((rows, heads * 2 * part), 1)
    first = (row // PAD) * (2 * part) + row % PAD
    real = row % PAD < part
    pairs = pairs_ref[...]
    x = dot(one_hot((item == first) & real), pairs)
    inv_rms = lax.rsqrt(jnp.sum(x * x, axis=1, keepdims=True) / width + 1e-06)
    normed = x * inv_rms
    scaled = moe[...] * gain_ref[...]
    mean = jnp.sum(scaled * normed, axis=1, keepdims=True) / width
    out_rows = dot(one_hot((item == first + part) & real), pairs)
    full = out_rows + inv_rms * (scaled - normed * mean)
    resid_ref[...] = full[:part].reshape(part, 1, width)
    product = dot_t(full.astype(BF), w_ref[...]).astype(BF)
    want = iota((heads * part, rows), 0)
    have = iota((heads * part, rows), 1)
    keep = one_hot(offset((want // part) ^ me, heads) * PAD + want % part == have)
    grad_ref[...] = dot(keep, product).astype(BF)


def call(kernel, out_shape, specs, flops, moved, scratch=(), out_specs=None, grant=GRANT):
    return pl.pallas_call(
        kernel,
        out_shape=out_shape,
        in_specs=specs,
        out_specs=out_specs or jax.tree.map(lambda _: VM, out_shape),
        scratch_shapes=scratch,
        cost_estimate=pl.CostEstimate(flops=flops, bytes_accessed=moved, transcendentals=0),
        compiler_params=pltpu.CompilerParams(vmem_limit_bytes=grant),
    )


def exchange(blocks, axis):
    return lax.all_to_all(blocks, axis, split_axis=0, concat_axis=0, tiled=True)


def shards(
    out_grad, layer_input, norm_gain, routes, gates, gate_pre, up_pre, w_gate, w_up, w_down, w_out
):
    experts_here = w_gate.shape[0]
    exp_groups = lax.axis_size("exp")
    quarters = lax.axis_size("seq")
    heads = lax.axis_size("head")
    capacity = gate_pre.shape[3]
    hidden = gate_pre.shape[4]
    tok_count, width = out_grad.shape
    piece = width // quarters
    part = tok_count // quarters
    block = experts_here * capacity
    rows = exp_groups * block
    attn = w_out.shape[0]
    packed = part * piece // LANES
    sds = jax.ShapeDtypeStruct
    quarter = lax.axis_index("seq").astype(I32).reshape(1)
    head = lax.axis_index("head").astype(I32).reshape(1)

    slots = call(
        functools.partial(dispatch_kernel, capacity),
        sds((rows, piece), BF),
        [SM, HB, HB, HB],
        2 * rows * tok_count * piece,
        1 << 20,
        [
            pltpu.VMEM(routes.T.shape, I32),
            pltpu.VMEM(gates.T.shape, F32),
            pltpu.VMEM((tok_count, piece), BF),
            DMA((3,)),
        ],
        grant=None,
    )(quarter, routes.T, gates.T, out_grad)

    received = exchange(slots.reshape(exp_groups, block, piece), "exp")

    downs = []
    for d in range(quarters):
        start = lax.rem(quarter[0] + d, quarters) * piece
        own = lax.dynamic_slice_in_dim(w_down, start, piece, 2)
        ring = [(i, (i + d) % quarters) for i in range(quarters)]
        downs.append(lax.ppermute(own, "seq", ring) if d else own)

    def own_rows(values):
        return lax.dynamic_slice_in_dim(values, quarter[0] * part, part, 0)

    def doubled(values, step):
        other = lax.ppermute(values, "head", [(i, i ^ step) for i in range(heads)])
        return jnp.concatenate([values, other], axis=0)

    pairs = jnp.concatenate([own_rows(layer_input), own_rows(out_grad)], axis=0)
    pairs = doubled(pairs, heads // 2)
    downs, pairs = lax.optimization_barrier((downs, pairs))

    partial_hidden = call(
        hidden_kernel,
        sds((quarters, experts_here * hidden, exp_groups * capacity), BF),
        [SM] + [VM] * (1 + quarters),
        2 * rows * width * hidden,
        3 << 20,
    )(quarter, received, *downs)
    summands = exchange(partial_hidden, "seq")
    parts = call(
        expert_kernel,
        sds((quarters, exp_groups, block, piece), BF),
        [VM] * 5,
        4 * rows * hidden * width,
        6 << 20,
        [pltpu.VMEM((quarters, exp_groups, block, piece), BF), DMA((quarters,))],
        HB,
    )(
        summands,
        gate_pre.reshape(experts_here, exp_groups * capacity, hidden),
        up_pre.reshape(experts_here, exp_groups * capacity, hidden),
        jnp.swapaxes(w_gate, 1, 2),
        jnp.swapaxes(w_up, 1, 2),
    )
    mine = exchange(parts, "seq")
    if heads > 2:
        pairs = doubled(pairs, heads // 4)
    mine, pairs = lax.optimization_barrier((mine, pairs))
    summed = call(
        sum_kernel, sds((exp_groups, block, piece), BF), [VM], 4 * rows * piece, 3 << 20
    )(mine)
    back = exchange(summed, "exp")
    step = heads // 8
    while step > 0:
        pairs = doubled(pairs, step)
        step //= 2
    late_routes, summed = lax.optimization_barrier((routes.T, summed))
    pick = call(
        functools.partial(pick_kernel, capacity),
        sds((tok_count, rows), BF),
        [VM],
        2 * rows * tok_count * tok_count,
        1 << 19,
    )(late_routes)
    back, pick, pairs = lax.optimization_barrier((back, pick, pairs))
    combined = call(
        combine_kernel,
        sds((quarters, heads, packed, LANES), BF),
        [VM] * 2,
        2 * rows * tok_count * piece,
        1 << 20,
    )(pick, back.reshape(rows, piece))
    got = exchange(combined.reshape(quarters * heads, packed, LANES), ("seq", "head"))
    resid, head_grad = call(
        finish_kernel,
        [sds((part, 1, width), F32), sds((heads * part, attn), BF)],
        [SM] + [VM] * 4,
        2 * heads * PAD * width * attn,
        4 << 20,
        [pltpu.VMEM((heads * PAD, width), F32)],
    )(
        head,
        got.reshape(quarters, heads, packed, LANES),
        pairs,
        norm_gain[None, :],
        w_out,
    )
    return jnp.swapaxes(resid, 0, 1), head_grad[None]


def solution(mesh):
    placed = (
        P(("exp", "head"), None),
        P(("exp", "head"), None),
        P(),
        P(("exp", "head"), None),
        P(("exp", "head"), None),
        P("head", "exp", None, None, "seq"),
        P("head", "exp", None, None, "seq"),
        P("exp", None, "seq"),
        P("exp", None, "seq"),
        P("exp", "seq", None),
        P("head", None),
    )
    return jax.shard_map(
        shards,
        mesh=mesh,
        in_specs=placed,
        out_specs=(P("seq", ("exp", "head"), None), P("seq", "exp", "head")),
        check_vma=False,
    )
```

```python
import functools

import jax
import jax.numpy as jnp
from jax import lax
from jax.experimental import pallas as pl
from jax.experimental.pallas import tpu as pltpu
from jax.sharding import PartitionSpec as P

BF = jnp.bfloat16
F32 = jnp.float32
I32 = jnp.int32
VM = pl.BlockSpec(memory_space=pltpu.VMEM)
SM = pl.BlockSpec(memory_space=pltpu.SMEM)
HB = pl.BlockSpec(memory_space=pltpu.HBM)
DMA = pltpu.SemaphoreType.DMA
PAD = 16
LANES = 128
GRANT = 12 << 20


def iota(shape, dim):
    return lax.broadcasted_iota(I32, shape, dim)


def one_hot(where):
    return jnp.where(where, 1.0, 0.0).astype(BF)


def dot(a, b):
    return jnp.dot(a, b, preferred_element_type=F32)


def dot_t(a, b):
    return lax.dot_general(a, b, (((1,), (1,)), ((), ())), preferred_element_type=F32)


def slot_hits(routes, capacity, rows, base=0):
    top, tok_count = routes.shape
    square = (tok_count, tok_count)
    earlier = one_hot(iota(square, 0) < iota(square, 1))
    row = base + iota((rows, tok_count), 0)
    hits = [routes[k : k + 1, :] == row // capacity for k in range(top)]
    named = jnp.zeros((rows, tok_count), F32)
    for hit in hits:
        named = jnp.where(hit, 1.0, named)
    count = dot(named.astype(BF), earlier)
    here = (named > 0.0) & (count == (row % capacity).astype(F32))
    return hits, here


def dispatch_kernel(
    capacity, quarter_ref, routes_hbm, gates_hbm, grad_hbm, slots_hbm, routes_ref, gates_ref, cols_ref, slots_ref, sems
):
    chunks, rows, piece = slots_ref.shape
    start = pl.multiple_of(quarter_ref[0] * piece, piece)
    copies = [
        pltpu.make_async_copy(routes_hbm, routes_ref, sems.at[0]),
        pltpu.make_async_copy(gates_hbm, gates_ref, sems.at[1]),
        pltpu.make_async_copy(grad_hbm.at[:, pl.ds(start, piece)], cols_ref, sems.at[2]),
    ]
    for copy in copies:
        copy.start()
    for copy in copies:
        copy.wait()
    outs = []
    for c in range(chunks):
        hits, here = slot_hits(routes_ref[...], capacity, rows, c * rows)
        gate = jnp.zeros(here.shape, F32)
        for k, hit in enumerate(hits):
            gate = jnp.where(hit, gates_ref[k : k + 1, :], gate)
        weight = jnp.sum(jnp.where(here, gate, 0.0), axis=1, keepdims=True)
        slots_ref[c] = (dot(one_hot(here), cols_ref[...]) * weight).astype(BF)
        outs.append(pltpu.make_async_copy(slots_ref.at[c], slots_hbm.at[c], sems.at[3 + c]))
        outs[-1].start()
    for copy in outs:
        copy.wait()


def pick_kernel(capacity, routes_ref, pick_ref):
    tok_count, rows = pick_ref.shape
    _, here = slot_hits(routes_ref[...], capacity, rows)
    square = (tok_count, tok_count)
    pick_ref[...] = dot_t(one_hot(iota(square, 0) == iota(square, 1)), one_hot(here)).astype(BF)


def hidden_kernel(quarter_ref, rows_ref, *refs):
    downs, out_ref = refs[:-1], refs[-1]
    groups, block, piece = rows_ref.shape
    experts_here, hidden, _ = downs[0].shape
    capacity = block // experts_here
    quarters = len(downs)
    wide = rows_ref[...].astype(F32)
    for j in range(experts_here):
        mine = wide[:, j * capacity : (j + 1) * capacity, :]
        mine = mine.reshape(groups * capacity, piece).astype(BF)
        for d in range(quarters):
            target = lax.rem(quarter_ref[0] + quarters - d, quarters)
            value = dot_t(downs[d][j], mine)
            out_ref[target, j * hidden : (j + 1) * hidden, :] = value.astype(BF)


def expert_kernel(parts_ref, gate_ref, up_ref, wg_ref, wu_ref, out_hbm, out, sems):
    quarters, groups, block, piece = out.shape
    experts_here, hidden, _ = wg_ref.shape
    capacity = block // experts_here
    grads = []
    for j in range(experts_here):
        band = slice(j * hidden, (j + 1) * hidden)
        total = parts_ref[0, band, :].astype(F32)
        for c in range(1, quarters):
            total = total + parts_ref[c, band, :].astype(F32)
        d_hidden = total.T
        act = gate_ref[j].astype(F32)
        up = up_ref[j].astype(F32)
        sig = jax.nn.sigmoid(act)
        d_gate = (d_hidden * up * (sig * (1.0 + act * (1.0 - sig)))).astype(BF)
        d_up = (d_hidden * (act * sig)).astype(BF)
        grads.append((d_gate, d_up))
    copies = []
    for c in range(quarters):
        cols = slice(c * piece, (c + 1) * piece)
        values = []
        for j in range(experts_here):
            value = dot(grads[j][0], wg_ref[j, :, cols]) + dot(grads[j][1], wu_ref[j, :, cols])
            values.append(value.reshape(groups, capacity, piece))
        out[c] = jnp.concatenate(values, axis=1).astype(BF)
        copies.append(pltpu.make_async_copy(out.at[c], out_hbm.at[c], sems.at[c]))
        copies[-1].start()
    for copy in copies:
        copy.wait()


def sum_kernel(parts_ref, out_hbm, out, sems):
    chunks = max(1, out.shape[0] // 8)
    copies = []
    for n in range(out.shape[0] // chunks):
        some = slice(n * chunks, (n + 1) * chunks)
        total = parts_ref[0, some].astype(F32)
        for c in range(1, parts_ref.shape[0]):
            total = total + parts_ref[c, some].astype(F32)
        out[some] = total.astype(BF)
        copies.append(pltpu.make_async_copy(out.at[some], out_hbm.at[some], sems.at[n]))
        copies[-1].start()
    for copy in copies:
        copy.wait()


def combine_kernel(pick_ref, back_ref, out_ref):
    quarters, heads, packed, lanes = out_ref.shape
    tok_count = pick_ref.shape[0]
    part = tok_count // quarters
    tiles = packed // part
    total = dot(pick_ref[...], back_ref[...]).astype(BF)
    stacked = jnp.concatenate([total[:, n * lanes : (n + 1) * lanes] for n in range(tiles)], axis=0)
    size = quarters * packed
    to = iota((size, size), 0)
    have = iota((size, size), 1)
    token = to // packed * part + to % part
    tile = to % packed // part
    value = dot(one_hot(have == tile * tok_count + token), stacked).astype(BF)
    for c in range(quarters):
        for h in range(heads):
            out_ref[c, h] = value[c * packed : (c + 1) * packed]


def offset(index, heads):
    turned = jnp.zeros_like(index)
    step = 1
    while step < heads:
        turned = turned * 2 + index // step % 2
        step *= 2
    return turned


def finish_kernel(head_ref, moe_ref, pairs_ref, gain_ref, w_ref, resid_ref, grad_ref, moe):
    quarters, heads, packed, lanes = moe_ref.shape
    part, _, width = resid_ref.shape
    tiles = packed // part
    piece = tiles * lanes
    rows = heads * PAD
    me = head_ref[0]
    row = iota((rows, heads * packed), 0)
    source = offset(row // PAD, heads) ^ me
    item = iota((rows, heads * packed), 1)
    for n in range(tiles):
        want = source * packed + n * part + row % PAD
        move = one_hot((want == item) & (row % PAD < part))
        blocks = [moe_ref[c].reshape(heads * packed, lanes) for c in range(quarters)]
        moved = dot(move, jnp.concatenate(blocks, axis=1))
        for c in range(quarters):
            start = c * piece + n * lanes
            moe[:, start : start + lanes] = moved[:, c * lanes : (c + 1) * lanes]
    both = pairs_ref[...].astype(F32).reshape(heads, 2 * part, width)
    x = both[:, :PAD].reshape(rows, width)
    tail = both[:, 8:PAD].reshape(heads * 8, width)
    tail = pltpu.roll(tail, heads * 8 - (PAD - part), 0).reshape(heads, 8, width)
    out_rows = jnp.concatenate([both[:, PAD:], tail], axis=1).reshape(rows, width)
    inv_rms = lax.rsqrt(jnp.sum(x * x, axis=1, keepdims=True) / width + 1e-06)
    normed = x * inv_rms
    scaled = moe[...] * gain_ref[...]
    mean = jnp.sum(scaled * normed, axis=1, keepdims=True) / width
    full = out_rows + inv_rms * (scaled - normed * mean)
    resid_ref[...] = full[:part].reshape(part, 1, width)
    product = dot_t(full.astype(BF), w_ref[...]).astype(BF)
    want = iota((heads * part, rows), 0)
    have = iota((heads * part, rows), 1)
    keep = one_hot(offset((want // part) ^ me, heads) * PAD + want % part == have)
    grad_ref[...] = dot(keep, product).astype(BF)


def call(kernel, out_shape, specs, flops, moved, scratch=(), out_specs=None, grant=GRANT):
    return pl.pallas_call(
        kernel,
        out_shape=out_shape,
        in_specs=specs,
        out_specs=out_specs or jax.tree.map(lambda _: VM, out_shape),
        scratch_shapes=scratch,
        cost_estimate=pl.CostEstimate(flops=flops, bytes_accessed=moved, transcendentals=0),
        compiler_params=pltpu.CompilerParams(vmem_limit_bytes=grant),
    )


def exchange(blocks, axis):
    return lax.all_to_all(blocks, axis, split_axis=0, concat_axis=0, tiled=True)


def shards(
    out_grad, layer_input, norm_gain, routes, gates, gate_pre, up_pre, w_gate, w_up, w_down, w_out
):
    experts_here = w_gate.shape[0]
    exp_groups = lax.axis_size("exp")
    quarters = lax.axis_size("seq")
    heads = lax.axis_size("head")
    capacity = gate_pre.shape[3]
    hidden = gate_pre.shape[4]
    tok_count, width = out_grad.shape
    piece = width // quarters
    part = tok_count // quarters
    block = experts_here * capacity
    rows = exp_groups * block
    attn = w_out.shape[0]
    packed = part * piece // LANES
    sds = jax.ShapeDtypeStruct
    quarter = lax.axis_index("seq").astype(I32).reshape(1)
    head = lax.axis_index("head").astype(I32).reshape(1)

    chunks = 4
    slots = call(
        functools.partial(dispatch_kernel, capacity),
        sds((chunks, rows // chunks, piece), BF),
        [SM, HB, HB, HB],
        2 * rows * tok_count * piece,
        1 << 20,
        [
            pltpu.VMEM(routes.T.shape, I32),
            pltpu.VMEM(gates.T.shape, F32),
            pltpu.VMEM((tok_count, piece), BF),
            pltpu.VMEM((chunks, rows // chunks, piece), BF),
            DMA((3 + chunks,)),
        ],
        HB,
        grant=None,
    )(quarter, routes.T, gates.T, out_grad)

    received = exchange(slots.reshape(exp_groups, block, piece), "exp")

    downs = []
    for d in range(quarters):
        start = lax.rem(quarter[0] + d, quarters) * piece
        own = lax.dynamic_slice_in_dim(w_down, start, piece, 2)
        ring = [(i, (i + d) % quarters) for i in range(quarters)]
        downs.append(lax.ppermute(own, "seq", ring) if d else own)

    def own_rows(values):
        return lax.dynamic_slice_in_dim(values, quarter[0] * part, part, 0)

    def doubled(values, step):
        other = lax.ppermute(values, "head", [(i, i ^ step) for i in range(heads)])
        return jnp.concatenate([values, other], axis=0)

    own_grad = own_rows(out_grad)
    pairs = jnp.concatenate([own_rows(layer_input), own_grad[8:], own_grad[:8]], axis=0)
    pairs = doubled(pairs, heads // 2)
    downs, pairs = lax.optimization_barrier((downs, pairs))

    partial_hidden = call(
        hidden_kernel,
        sds((quarters, experts_here * hidden, exp_groups * capacity), BF),
        [SM] + [VM] * (1 + quarters),
        2 * rows * width * hidden,
        3 << 20,
    )(quarter, received, *downs)
    summands = exchange(partial_hidden, "seq")
    parts = call(
        expert_kernel,
        sds((quarters, exp_groups, block, piece), BF),
        [VM] * 5,
        4 * rows * hidden * width,
        6 << 20,
        [pltpu.VMEM((quarters, exp_groups, block, piece), BF), DMA((quarters,))],
        HB,
    )(
        summands,
        gate_pre.reshape(experts_here, exp_groups * capacity, hidden),
        up_pre.reshape(experts_here, exp_groups * capacity, hidden),
        jnp.swapaxes(w_gate, 1, 2),
        jnp.swapaxes(w_up, 1, 2),
    )
    mine = exchange(parts, "seq")
    if heads > 2:
        pairs = doubled(pairs, heads // 4)
    mine, pairs = lax.optimization_barrier((mine, pairs))
    summed = call(
        sum_kernel,
        sds((exp_groups, block, piece), BF),
        [VM],
        4 * rows * piece,
        3 << 20,
        [pltpu.VMEM((exp_groups, block, piece), BF), DMA((exp_groups // max(1, exp_groups // 8),))],
        HB,
    )(mine)
    back = exchange(summed, "exp")
    step = heads // 8
    while step > 0:
        pairs = doubled(pairs, step)
        step //= 2
    late_routes, summed = lax.optimization_barrier((routes.T, summed))
    pick = call(
        functools.partial(pick_kernel, capacity),
        sds((tok_count, rows), BF),
        [VM],
        2 * rows * tok_count * tok_count,
        1 << 19,
    )(late_routes)
    back, pick, pairs = lax.optimization_barrier((back, pick, pairs))
    combined = call(
        combine_kernel,
        sds((quarters, heads, packed, LANES), BF),
        [VM] * 2,
        2 * rows * tok_count * piece,
        1 << 20,
    )(pick, back.reshape(rows, piece))
    got = exchange(combined.reshape(quarters * heads, packed, LANES), ("seq", "head"))
    resid, head_grad = call(
        finish_kernel,
        [sds((part, 1, width), F32), sds((heads * part, attn), BF)],
        [SM] + [VM] * 4,
        2 * heads * PAD * width * attn,
        4 << 20,
        [pltpu.VMEM((heads * PAD, width), F32)],
    )(
        head,
        got.reshape(quarters, heads, packed, LANES),
        pairs,
        norm_gain[None, :],
        w_out,
    )
    return jnp.swapaxes(resid, 0, 1), head_grad[None]


def solution(mesh):
    placed = (
        P(("exp", "head"), None),
        P(("exp", "head"), None),
        P(),
        P(("exp", "head"), None),
        P(("exp", "head"), None),
        P("head", "exp", None, None, "seq"),
        P("head", "exp", None, None, "seq"),
        P("exp", None, "seq"),
        P("exp", None, "seq"),
        P("exp", "seq", None),
        P("head", None),
    )
    return jax.shard_map(
        shards,
        mesh=mesh,
        in_specs=placed,
        out_specs=(P("seq", ("exp", "head"), None), P("seq", "exp", "head")),
        check_vma=False,
    )
```

```python
import functools

import jax
import jax.numpy as jnp
from jax import lax
from jax.experimental import pallas as pl
from jax.experimental.pallas import tpu as pltpu
from jax.sharding import PartitionSpec as P

BF = jnp.bfloat16
F32 = jnp.float32
I32 = jnp.int32
VM = pl.BlockSpec(memory_space=pltpu.VMEM)
SM = pl.BlockSpec(memory_space=pltpu.SMEM)
HB = pl.BlockSpec(memory_space=pltpu.HBM)
DMA = pltpu.SemaphoreType.DMA
PAD = 16
LANES = 128
GRANT = 12 << 20


def iota(shape, dim):
    return lax.broadcasted_iota(I32, shape, dim)


def one_hot(where):
    return jnp.where(where, 1.0, 0.0).astype(BF)


def dot(a, b):
    return jnp.dot(a, b, preferred_element_type=F32)


def dot_t(a, b):
    return lax.dot_general(a, b, (((1,), (1,)), ((), ())), preferred_element_type=F32)


def slot_hits(routes, capacity, rows, base=0):
    top, tok_count = routes.shape
    square = (tok_count, tok_count)
    earlier = one_hot(iota(square, 0) < iota(square, 1))
    row = base + iota((rows, tok_count), 0)
    hits = [routes[k : k + 1, :] == row // capacity for k in range(top)]
    named = jnp.zeros((rows, tok_count), F32)
    for hit in hits:
        named = jnp.where(hit, 1.0, named)
    count = dot(named.astype(BF), earlier)
    here = (named > 0.0) & (count == (row % capacity).astype(F32))
    return hits, here


def dispatch_kernel(
    capacity, quarter_ref, routes_hbm, gates_hbm, grad_hbm, slots_hbm, routes_ref, gates_ref, cols_ref, slots_ref, sems
):
    chunks, rows, piece = slots_ref.shape
    start = pl.multiple_of(quarter_ref[0] * piece, piece)
    copies = [
        pltpu.make_async_copy(routes_hbm, routes_ref, sems.at[0]),
        pltpu.make_async_copy(gates_hbm, gates_ref, sems.at[1]),
        pltpu.make_async_copy(grad_hbm.at[:, pl.ds(start, piece)], cols_ref, sems.at[2]),
    ]
    for copy in copies:
        copy.start()
    for copy in copies:
        copy.wait()
    outs = []
    for c in range(chunks):
        hits, here = slot_hits(routes_ref[...], capacity, rows, c * rows)
        gate = jnp.zeros(here.shape, F32)
        for k, hit in enumerate(hits):
            gate = jnp.where(hit, gates_ref[k : k + 1, :], gate)
        weight = jnp.sum(jnp.where(here, gate, 0.0), axis=1, keepdims=True)
        slots_ref[c] = (dot(one_hot(here), cols_ref[...]) * weight).astype(BF)
        outs.append(pltpu.make_async_copy(slots_ref.at[c], slots_hbm.at[c], sems.at[3 + c]))
        outs[-1].start()
    for copy in outs:
        copy.wait()


def pick_kernel(capacity, routes_ref, pick_ref):
    tok_count, rows = pick_ref.shape
    _, here = slot_hits(routes_ref[...], capacity, rows)
    square = (tok_count, tok_count)
    pick_ref[...] = dot_t(one_hot(iota(square, 0) == iota(square, 1)), one_hot(here)).astype(BF)


def hidden_kernel(quarter_ref, rows_ref, *refs):
    downs, out_ref = refs[:-1], refs[-1]
    groups, block, piece = rows_ref.shape
    experts_here, hidden, _ = downs[0].shape
    capacity = block // experts_here
    quarters = len(downs)
    own = pl.ds(pl.multiple_of(quarter_ref[0] * piece, piece), piece)
    wide = rows_ref[...].astype(F32)
    for j in range(experts_here):
        mine = wide[:, j * capacity : (j + 1) * capacity, :]
        mine = mine.reshape(groups * capacity, piece).astype(BF)
        for d in range(quarters):
            target = lax.rem(quarter_ref[0] + quarters - d, quarters)
            value = dot_t(downs[d][j] if d else downs[0][j, :, own], mine)
            out_ref[target, j * hidden : (j + 1) * hidden, :] = value.astype(BF)


def expert_kernel(parts_ref, gate_ref, up_ref, wg_ref, wu_ref, out_hbm, out, sems):
    quarters, groups, block, piece = out.shape
    experts_here, hidden, _ = wg_ref.shape
    capacity = block // experts_here
    grads = []
    for j in range(experts_here):
        band = slice(j * hidden, (j + 1) * hidden)
        total = parts_ref[0, band, :].astype(F32)
        for c in range(1, quarters):
            total = total + parts_ref[c, band, :].astype(F32)
        d_hidden = total.T
        act = gate_ref[j].astype(F32)
        up = up_ref[j].astype(F32)
        sig = jax.nn.sigmoid(act)
        d_gate = (d_hidden * up * (sig * (1.0 + act * (1.0 - sig)))).astype(BF)
        d_up = (d_hidden * (act * sig)).astype(BF)
        grads.append((d_gate, d_up))
    copies = []
    for c in range(quarters):
        cols = slice(c * piece, (c + 1) * piece)
        values = []
        for j in range(experts_here):
            value = dot(grads[j][0], wg_ref[j, :, cols]) + dot(grads[j][1], wu_ref[j, :, cols])
            values.append(value.reshape(groups, capacity, piece))
        out[c] = jnp.concatenate(values, axis=1).astype(BF)
        copies.append(pltpu.make_async_copy(out.at[c], out_hbm.at[c], sems.at[c]))
        copies[-1].start()
    for copy in copies:
        copy.wait()


def sum_kernel(parts_ref, out_hbm, out, sems):
    chunks = max(1, out.shape[0] // 8)
    copies = []
    for n in range(out.shape[0] // chunks):
        some = slice(n * chunks, (n + 1) * chunks)
        total = parts_ref[0, some].astype(F32)
        for c in range(1, parts_ref.shape[0]):
            total = total + parts_ref[c, some].astype(F32)
        out[some] = total.astype(BF)
        copies.append(pltpu.make_async_copy(out.at[some], out_hbm.at[some], sems.at[n]))
        copies[-1].start()
    for copy in copies:
        copy.wait()


def combine_kernel(pick_ref, back_ref, out_ref):
    quarters, heads, packed, lanes = out_ref.shape
    tok_count = pick_ref.shape[0]
    part = tok_count // quarters
    tiles = packed // part
    total = dot(pick_ref[...], back_ref[...]).astype(BF)
    stacked = jnp.concatenate([total[:, n * lanes : (n + 1) * lanes] for n in range(tiles)], axis=0)
    size = quarters * packed
    to = iota((size, size), 0)
    have = iota((size, size), 1)
    token = to // packed * part + to % part
    tile = to % packed // part
    value = dot(one_hot(have == tile * tok_count + token), stacked).astype(BF)
    for c in range(quarters):
        for h in range(heads):
            out_ref[c, h] = value[c * packed : (c + 1) * packed]


def offset(index, heads):
    turned = jnp.zeros_like(index)
    step = 1
    while step < heads:
        turned = turned * 2 + index // step % 2
        step *= 2
    return turned


def finish_kernel(head_ref, moe_ref, pairs_ref, gain_ref, w_ref, resid_ref, grad_ref, moe):
    quarters, heads, packed, lanes = moe_ref.shape
    part, _, width = resid_ref.shape
    tiles = packed // part
    piece = tiles * lanes
    rows = heads * PAD
    me = head_ref[0]
    row = iota((rows, heads * packed), 0)
    source = offset(row // PAD, heads) ^ me
    item = iota((rows, heads * packed), 1)
    for n in range(tiles):
        want = source * packed + n * part + row % PAD
        move = one_hot((want == item) & (row % PAD < part))
        blocks = [moe_ref[c].reshape(heads * packed, lanes) for c in range(quarters)]
        moved = dot(move, jnp.concatenate(blocks, axis=1))
        for c in range(quarters):
            start = c * piece + n * lanes
            moe[:, start : start + lanes] = moved[:, c * lanes : (c + 1) * lanes]
    both = pairs_ref[...].astype(F32).reshape(heads, 2 * part, width)
    x = both[:, :PAD].reshape(rows, width)
    tail = both[:, 8:PAD].reshape(heads * 8, width)
    tail = pltpu.roll(tail, heads * 8 - (PAD - part), 0).reshape(heads, 8, width)
    out_rows = jnp.concatenate([both[:, PAD:], tail], axis=1).reshape(rows, width)
    inv_rms = lax.rsqrt(jnp.sum(x * x, axis=1, keepdims=True) / width + 1e-06)
    normed = x * inv_rms
    scaled = moe[...] * gain_ref[...]
    mean = jnp.sum(scaled * normed, axis=1, keepdims=True) / width
    full = out_rows + inv_rms * (scaled - normed * mean)
    resid_ref[...] = full[:part].reshape(part, 1, width)
    product = dot_t(full.astype(BF), w_ref[...]).astype(BF)
    want = iota((heads * part, rows), 0)
    have = iota((heads * part, rows), 1)
    keep = one_hot(offset((want // part) ^ me, heads) * PAD + want % part == have)
    grad_ref[...] = dot(keep, product).astype(BF)


def call(kernel, out_shape, specs, flops, moved, scratch=(), out_specs=None, grant=GRANT):
    return pl.pallas_call(
        kernel,
        out_shape=out_shape,
        in_specs=specs,
        out_specs=out_specs or jax.tree.map(lambda _: VM, out_shape),
        scratch_shapes=scratch,
        cost_estimate=pl.CostEstimate(flops=flops, bytes_accessed=moved, transcendentals=0),
        compiler_params=pltpu.CompilerParams(vmem_limit_bytes=grant),
    )


def exchange(blocks, axis):
    return lax.all_to_all(blocks, axis, split_axis=0, concat_axis=0, tiled=True)


def shards(
    out_grad, layer_input, norm_gain, routes, gates, gate_pre, up_pre, w_gate, w_up, w_down, w_out
):
    experts_here = w_gate.shape[0]
    exp_groups = lax.axis_size("exp")
    quarters = lax.axis_size("seq")
    heads = lax.axis_size("head")
    capacity = gate_pre.shape[3]
    hidden = gate_pre.shape[4]
    tok_count, width = out_grad.shape
    piece = width // quarters
    part = tok_count // quarters
    block = experts_here * capacity
    rows = exp_groups * block
    attn = w_out.shape[0]
    packed = part * piece // LANES
    sds = jax.ShapeDtypeStruct
    quarter = lax.axis_index("seq").astype(I32).reshape(1)
    head = lax.axis_index("head").astype(I32).reshape(1)

    chunks = 4
    slots = call(
        functools.partial(dispatch_kernel, capacity),
        sds((chunks, rows // chunks, piece), BF),
        [SM, HB, HB, HB],
        2 * rows * tok_count * piece,
        1 << 20,
        [
            pltpu.VMEM(routes.T.shape, I32),
            pltpu.VMEM(gates.T.shape, F32),
            pltpu.VMEM((tok_count, piece), BF),
            pltpu.VMEM((chunks, rows // chunks, piece), BF),
            DMA((3 + chunks,)),
        ],
        HB,
        grant=None,
    )(quarter, routes.T, gates.T, out_grad)

    received = exchange(slots.reshape(exp_groups, block, piece), "exp")

    downs = [w_down]
    for d in range(1, quarters):
        start = lax.rem(quarter[0] + d, quarters) * piece
        own = lax.dynamic_slice_in_dim(w_down, start, piece, 2)
        ring = [(i, (i + d) % quarters) for i in range(quarters)]
        downs.append(lax.ppermute(own, "seq", ring))

    def own_rows(values):
        return lax.dynamic_slice_in_dim(values, quarter[0] * part, part, 0)

    def doubled(values, step):
        other = lax.ppermute(values, "head", [(i, i ^ step) for i in range(heads)])
        return jnp.concatenate([values, other], axis=0)

    own_grad = own_rows(out_grad)
    pairs = jnp.concatenate([own_rows(layer_input), own_grad[8:], own_grad[:8]], axis=0)

    partial_hidden = call(
        hidden_kernel,
        sds((quarters, experts_here * hidden, exp_groups * capacity), BF),
        [SM] + [VM] * (1 + quarters),
        2 * rows * width * hidden,
        3 << 20,
    )(quarter, received, *downs)
    summands = exchange(partial_hidden, "seq")
    parts = call(
        expert_kernel,
        sds((quarters, exp_groups, block, piece), BF),
        [VM] * 5,
        4 * rows * hidden * width,
        6 << 20,
        [pltpu.VMEM((quarters, exp_groups, block, piece), BF), DMA((quarters,))],
        HB,
    )(
        summands,
        gate_pre.reshape(experts_here, exp_groups * capacity, hidden),
        up_pre.reshape(experts_here, exp_groups * capacity, hidden),
        jnp.swapaxes(w_gate, 1, 2),
        jnp.swapaxes(w_up, 1, 2),
    )
    mine = exchange(parts, "seq")
    pairs = doubled(pairs, heads // 2)
    mine, pairs = lax.optimization_barrier((mine, pairs))
    summed = call(
        sum_kernel,
        sds((exp_groups, block, piece), BF),
        [VM],
        4 * rows * piece,
        3 << 20,
        [pltpu.VMEM((exp_groups, block, piece), BF), DMA((exp_groups // max(1, exp_groups // 8),))],
        HB,
    )(mine)
    back = exchange(summed, "exp")
    step = heads // 4
    while step > 0:
        pairs = doubled(pairs, step)
        step //= 2
    late_routes, summed = lax.optimization_barrier((routes.T, summed))
    pick = call(
        functools.partial(pick_kernel, capacity),
        sds((tok_count, rows), BF),
        [VM],
        2 * rows * tok_count * tok_count,
        1 << 19,
    )(late_routes)
    back, pick, pairs = lax.optimization_barrier((back, pick, pairs))
    combined = call(
        combine_kernel,
        sds((quarters, heads, packed, LANES), BF),
        [VM] * 2,
        2 * rows * tok_count * piece,
        1 << 20,
    )(pick, back.reshape(rows, piece))
    got = exchange(combined.reshape(quarters * heads, packed, LANES), ("seq", "head"))
    resid, head_grad = call(
        finish_kernel,
        [sds((part, 1, width), F32), sds((heads * part, attn), BF)],
        [SM] + [VM] * 4,
        2 * heads * PAD * width * attn,
        4 << 20,
        [pltpu.VMEM((heads * PAD, width), F32)],
    )(
        head,
        got.reshape(quarters, heads, packed, LANES),
        pairs,
        norm_gain[None, :],
        w_out,
    )
    return jnp.swapaxes(resid, 0, 1), head_grad[None]


def solution(mesh):
    placed = (
        P(("exp", "head"), None),
        P(("exp", "head"), None),
        P(),
        P(("exp", "head"), None),
        P(("exp", "head"), None),
        P("head", "exp", None, None, "seq"),
        P("head", "exp", None, None, "seq"),
        P("exp", None, "seq"),
        P("exp", None, "seq"),
        P("exp", "seq", None),
        P("head", None),
    )
    return jax.shard_map(
        shards,
        mesh=mesh,
        in_specs=placed,
        out_specs=(P("seq", ("exp", "head"), None), P("seq", "exp", "head")),
        check_vma=False,
    )
```

```python
import functools

import jax
import jax.numpy as jnp
from jax import lax
from jax.experimental import pallas as pl
from jax.experimental.pallas import tpu as pltpu
from jax.sharding import PartitionSpec as P

BF = jnp.bfloat16
F32 = jnp.float32
I32 = jnp.int32
VM = pl.BlockSpec(memory_space=pltpu.VMEM)
SM = pl.BlockSpec(memory_space=pltpu.SMEM)
HB = pl.BlockSpec(memory_space=pltpu.HBM)
DMA = pltpu.SemaphoreType.DMA
PAD = 16
LANES = 128
GRANT = 12 << 20


def iota(shape, dim):
    return lax.broadcasted_iota(I32, shape, dim)


def one_hot(where):
    return jnp.where(where, 1.0, 0.0).astype(BF)


def dot(a, b):
    return jnp.dot(a, b, preferred_element_type=F32)


def dot_t(a, b):
    return lax.dot_general(a, b, (((1,), (1,)), ((), ())), preferred_element_type=F32)


def slot_hits(routes, capacity, rows, base=0):
    top, tok_count = routes.shape
    square = (tok_count, tok_count)
    earlier = one_hot(iota(square, 0) < iota(square, 1))
    row = base + iota((rows, tok_count), 0)
    hits = [routes[k : k + 1, :] == row // capacity for k in range(top)]
    named = jnp.zeros((rows, tok_count), F32)
    for hit in hits:
        named = jnp.where(hit, 1.0, named)
    count = dot(named.astype(BF), earlier)
    here = (named > 0.0) & (count == (row % capacity).astype(F32))
    return hits, here


def dispatch_kernel(
    capacity, quarter_ref, routes_hbm, gates_hbm, grad_hbm, slots_hbm, routes_ref, gates_ref, cols_ref, slots_ref, sems
):
    chunks, rows, piece = slots_ref.shape
    start = pl.multiple_of(quarter_ref[0] * piece, piece)
    copies = [
        pltpu.make_async_copy(routes_hbm, routes_ref, sems.at[0]),
        pltpu.make_async_copy(gates_hbm, gates_ref, sems.at[1]),
        pltpu.make_async_copy(grad_hbm.at[:, pl.ds(start, piece)], cols_ref, sems.at[2]),
    ]
    for copy in copies:
        copy.start()
    for copy in copies:
        copy.wait()
    outs = []
    for c in range(chunks):
        hits, here = slot_hits(routes_ref[...], capacity, rows, c * rows)
        gate = jnp.zeros(here.shape, F32)
        for k, hit in enumerate(hits):
            gate = jnp.where(hit, gates_ref[k : k + 1, :], gate)
        weight = jnp.sum(jnp.where(here, gate, 0.0), axis=1, keepdims=True)
        slots_ref[c] = (dot(one_hot(here), cols_ref[...]) * weight).astype(BF)
        outs.append(pltpu.make_async_copy(slots_ref.at[c], slots_hbm.at[c], sems.at[3 + c]))
        outs[-1].start()
    for copy in outs:
        copy.wait()


def pick_kernel(capacity, routes_ref, pick_ref):
    tok_count, rows = pick_ref.shape
    _, here = slot_hits(routes_ref[...], capacity, rows)
    square = (tok_count, tok_count)
    pick_ref[...] = dot_t(one_hot(iota(square, 0) == iota(square, 1)), one_hot(here)).astype(BF)


def hidden_kernel(quarter_ref, rows_ref, *refs):
    downs, out_ref = refs[:-1], refs[-1]
    groups, block, piece = rows_ref.shape
    experts_here, hidden, _ = downs[0].shape
    capacity = block // experts_here
    quarters = len(downs)
    own = pl.ds(pl.multiple_of(quarter_ref[0] * piece, piece), piece)
    wide = rows_ref[...].astype(F32)
    for j in range(experts_here):
        mine = wide[:, j * capacity : (j + 1) * capacity, :]
        mine = mine.reshape(groups * capacity, piece).astype(BF)
        for d in range(quarters):
            target = lax.rem(quarter_ref[0] + quarters - d, quarters)
            value = dot_t(downs[d][j] if d else downs[0][j, :, own], mine)
            out_ref[target, j * hidden : (j + 1) * hidden, :] = value.astype(BF)


def expert_kernel(parts_ref, gate_ref, up_ref, wg_ref, wu_ref, out_hbm, out, sems):
    quarters, groups, block, piece = out.shape
    experts_here, hidden, _ = wg_ref.shape
    capacity = block // experts_here
    grads = []
    for j in range(experts_here):
        band = slice(j * hidden, (j + 1) * hidden)
        total = parts_ref[0, band, :].astype(F32)
        for c in range(1, quarters):
            total = total + parts_ref[c, band, :].astype(F32)
        d_hidden = total.T
        act = gate_ref[j].astype(F32)
        up = up_ref[j].astype(F32)
        sig = jax.nn.sigmoid(act)
        d_gate = (d_hidden * up * (sig * (1.0 + act * (1.0 - sig)))).astype(BF)
        d_up = (d_hidden * (act * sig)).astype(BF)
        grads.append((d_gate, d_up))
    copies = []
    for c in range(quarters):
        cols = slice(c * piece, (c + 1) * piece)
        values = []
        for j in range(experts_here):
            value = dot(grads[j][0], wg_ref[j, :, cols]) + dot(grads[j][1], wu_ref[j, :, cols])
            values.append(value.reshape(groups, capacity, piece))
        out[c] = jnp.concatenate(values, axis=1).astype(BF)
        copies.append(pltpu.make_async_copy(out.at[c], out_hbm.at[c], sems.at[c]))
        copies[-1].start()
    for copy in copies:
        copy.wait()


def sum_kernel(parts_ref, out_hbm, out, sems):
    chunks = max(1, out.shape[0] // 8)
    copies = []
    for n in range(out.shape[0] // chunks):
        some = slice(n * chunks, (n + 1) * chunks)
        total = parts_ref[0, some].astype(F32)
        for c in range(1, parts_ref.shape[0]):
            total = total + parts_ref[c, some].astype(F32)
        out[some] = total.astype(BF)
        copies.append(pltpu.make_async_copy(out.at[some], out_hbm.at[some], sems.at[n]))
        copies[-1].start()
    for copy in copies:
        copy.wait()


def combine_kernel(pick_ref, back_ref, out_ref):
    quarters, heads, packed, lanes = out_ref.shape
    tok_count = pick_ref.shape[0]
    part = tok_count // quarters
    tiles = packed // part
    total = dot(pick_ref[...], back_ref[...]).astype(BF)
    stacked = jnp.concatenate([total[:, n * lanes : (n + 1) * lanes] for n in range(tiles)], axis=0)
    size = quarters * packed
    to = iota((size, size), 0)
    have = iota((size, size), 1)
    token = to // packed * part + to % part
    tile = to % packed // part
    value = dot(one_hot(have == tile * tok_count + token), stacked).astype(BF)
    for c in range(quarters):
        for h in range(heads):
            out_ref[c, h] = value[c * packed : (c + 1) * packed]


def offset(index, heads):
    turned = jnp.zeros_like(index)
    step = 1
    while step < heads:
        turned = turned * 2 + index // step % 2
        step *= 2
    return turned


def finish_kernel(
    head_ref, moe_ref, near_ref, far_hbm, gain_ref, w_ref, resid_ref, grad_ref, moe, far_ref, sem
):
    far_copy = pltpu.make_async_copy(far_hbm, far_ref, sem.at[0])
    far_copy.start()
    quarters, heads, packed, lanes = moe_ref.shape
    part, _, width = resid_ref.shape
    tiles = packed // part
    piece = tiles * lanes
    rows = heads * PAD
    me = head_ref[0]
    row = iota((rows, heads * packed), 0)
    source = offset(row // PAD, heads) ^ me
    item = iota((rows, heads * packed), 1)
    for n in range(tiles):
        want = source * packed + n * part + row % PAD
        move = one_hot((want == item) & (row % PAD < part))
        blocks = [moe_ref[c].reshape(heads * packed, lanes) for c in range(quarters)]
        moved = dot(move, jnp.concatenate(blocks, axis=1))
        for c in range(quarters):
            start = c * piece + n * lanes
            moe[:, start : start + lanes] = moved[:, c * lanes : (c + 1) * lanes]
    far_copy.wait()
    halves = [ref[...].astype(F32).reshape(heads // 2, 2 * part, width) for ref in (near_ref, far_ref)]
    both = jnp.concatenate(halves, axis=0)
    x = both[:, :PAD].reshape(rows, width)
    tail = both[:, 8:PAD].reshape(heads * 8, width)
    tail = pltpu.roll(tail, heads * 8 - (PAD - part), 0).reshape(heads, 8, width)
    out_rows = jnp.concatenate([both[:, PAD:], tail], axis=1).reshape(rows, width)
    inv_rms = lax.rsqrt(jnp.sum(x * x, axis=1, keepdims=True) / width + 1e-06)
    normed = x * inv_rms
    scaled = moe[...] * gain_ref[...]
    mean = jnp.sum(scaled * normed, axis=1, keepdims=True) / width
    full = out_rows + inv_rms * (scaled - normed * mean)
    resid_ref[...] = full[:part].reshape(part, 1, width)
    product = dot_t(full.astype(BF), w_ref[...]).astype(BF)
    want = iota((heads * part, rows), 0)
    have = iota((heads * part, rows), 1)
    keep = one_hot(offset((want // part) ^ me, heads) * PAD + want % part == have)
    grad_ref[...] = dot(keep, product).astype(BF)


def call(kernel, out_shape, specs, flops, moved, scratch=(), out_specs=None, grant=GRANT):
    return pl.pallas_call(
        kernel,
        out_shape=out_shape,
        in_specs=specs,
        out_specs=out_specs or jax.tree.map(lambda _: VM, out_shape),
        scratch_shapes=scratch,
        cost_estimate=pl.CostEstimate(flops=flops, bytes_accessed=moved, transcendentals=0),
        compiler_params=pltpu.CompilerParams(vmem_limit_bytes=grant),
    )


def exchange(blocks, axis):
    return lax.all_to_all(blocks, axis, split_axis=0, concat_axis=0, tiled=True)


def shards(
    out_grad, layer_input, norm_gain, routes, gates, gate_pre, up_pre, w_gate, w_up, w_down, w_out
):
    experts_here = w_gate.shape[0]
    exp_groups = lax.axis_size("exp")
    quarters = lax.axis_size("seq")
    heads = lax.axis_size("head")
    capacity = gate_pre.shape[3]
    hidden = gate_pre.shape[4]
    tok_count, width = out_grad.shape
    piece = width // quarters
    part = tok_count // quarters
    block = experts_here * capacity
    rows = exp_groups * block
    attn = w_out.shape[0]
    packed = part * piece // LANES
    sds = jax.ShapeDtypeStruct
    quarter = lax.axis_index("seq").astype(I32).reshape(1)
    head = lax.axis_index("head").astype(I32).reshape(1)

    chunks = 4
    slots = call(
        functools.partial(dispatch_kernel, capacity),
        sds((chunks, rows // chunks, piece), BF),
        [SM, HB, HB, HB],
        2 * rows * tok_count * piece,
        1 << 20,
        [
            pltpu.VMEM(routes.T.shape, I32),
            pltpu.VMEM(gates.T.shape, F32),
            pltpu.VMEM((tok_count, piece), BF),
            pltpu.VMEM((chunks, rows // chunks, piece), BF),
            DMA((3 + chunks,)),
        ],
        HB,
        grant=None,
    )(quarter, routes.T, gates.T, out_grad)

    received = exchange(slots.reshape(exp_groups, block, piece), "exp")

    downs = [w_down]
    for d in range(1, quarters):
        start = lax.rem(quarter[0] + d, quarters) * piece
        own = lax.dynamic_slice_in_dim(w_down, start, piece, 2)
        ring = [(i, (i + d) % quarters) for i in range(quarters)]
        downs.append(lax.ppermute(own, "seq", ring))

    def own_rows(values):
        return lax.dynamic_slice_in_dim(values, quarter[0] * part, part, 0)

    def doubled(values, step):
        other = lax.ppermute(values, "head", [(i, i ^ step) for i in range(heads)])
        return jnp.concatenate([values, other], axis=0)

    own_grad = own_rows(out_grad)
    pairs = jnp.concatenate([own_rows(layer_input), own_grad[8:], own_grad[:8]], axis=0)

    partial_hidden = call(
        hidden_kernel,
        sds((quarters, experts_here * hidden, exp_groups * capacity), BF),
        [SM] + [VM] * (1 + quarters),
        2 * rows * width * hidden,
        3 << 20,
    )(quarter, received, *downs)
    summands = exchange(partial_hidden, "seq")
    parts = call(
        expert_kernel,
        sds((quarters, exp_groups, block, piece), BF),
        [VM] * 5,
        4 * rows * hidden * width,
        6 << 20,
        [pltpu.VMEM((quarters, exp_groups, block, piece), BF), DMA((quarters,))],
        HB,
    )(
        summands,
        gate_pre.reshape(experts_here, exp_groups * capacity, hidden),
        up_pre.reshape(experts_here, exp_groups * capacity, hidden),
        jnp.swapaxes(w_gate, 1, 2),
        jnp.swapaxes(w_up, 1, 2),
    )
    mine = exchange(parts, "seq")
    pairs = doubled(pairs, heads // 2)
    mine, pairs = lax.optimization_barrier((mine, pairs))
    summed = call(
        sum_kernel,
        sds((exp_groups, block, piece), BF),
        [VM],
        4 * rows * piece,
        3 << 20,
        [pltpu.VMEM((exp_groups, block, piece), BF), DMA((exp_groups // max(1, exp_groups // 8),))],
        HB,
    )(mine)
    back = exchange(summed, "exp")
    step = heads // 4
    while step > 1:
        pairs = doubled(pairs, step)
        step //= 2
    far = lax.ppermute(pairs, "head", [(i, i ^ 1) for i in range(heads)])
    late_routes, summed = lax.optimization_barrier((routes.T, summed))
    pick = call(
        functools.partial(pick_kernel, capacity),
        sds((tok_count, rows), BF),
        [VM],
        2 * rows * tok_count * tok_count,
        1 << 19,
    )(late_routes)
    back, pick, pairs, far, head = lax.optimization_barrier((back, pick, pairs, far, head))
    combined = call(
        combine_kernel,
        sds((quarters, heads, packed, LANES), BF),
        [VM] * 2,
        2 * rows * tok_count * piece,
        1 << 20,
    )(pick, back.reshape(rows, piece))
    got = exchange(combined.reshape(quarters * heads, packed, LANES), ("seq", "head"))
    resid, head_grad = call(
        finish_kernel,
        [sds((part, 1, width), F32), sds((heads * part, attn), BF)],
        [SM, VM, VM, HB, VM, VM],
        2 * heads * PAD * width * attn,
        4 << 20,
        [pltpu.VMEM((heads * PAD, width), F32), pltpu.VMEM(far.shape, BF), DMA((1,))],
    )(
        head,
        got.reshape(quarters, heads, packed, LANES),
        pairs,
        far,
        norm_gain[None, :],
        w_out,
    )
    return jnp.swapaxes(resid, 0, 1), head_grad[None]


def solution(mesh):
    placed = (
        P(("exp", "head"), None),
        P(("exp", "head"), None),
        P(),
        P(("exp", "head"), None),
        P(("exp", "head"), None),
        P("head", "exp", None, None, "seq"),
        P("head", "exp", None, None, "seq"),
        P("exp", None, "seq"),
        P("exp", None, "seq"),
        P("exp", "seq", None),
        P("head", None),
    )
    return jax.shard_map(
        shards,
        mesh=mesh,
        in_specs=placed,
        out_specs=(P("seq", ("exp", "head"), None), P("seq", "exp", "head")),
        check_vma=False,
    )
```

```python
import functools

import jax
import jax.numpy as jnp
from jax import lax
from jax.experimental import pallas as pl
from jax.experimental.pallas import tpu as pltpu
from jax.sharding import PartitionSpec as P

BF = jnp.bfloat16
F32 = jnp.float32
I32 = jnp.int32
VM = pl.BlockSpec(memory_space=pltpu.VMEM)
SM = pl.BlockSpec(memory_space=pltpu.SMEM)
HB = pl.BlockSpec(memory_space=pltpu.HBM)
DMA = pltpu.SemaphoreType.DMA
PAD = 16
LANES = 128
GRANT = 12 << 20


def iota(shape, dim):
    return lax.broadcasted_iota(I32, shape, dim)


def one_hot(where):
    return jnp.where(where, 1.0, 0.0).astype(BF)


def dot(a, b):
    return jnp.dot(a, b, preferred_element_type=F32)


def dot_t(a, b):
    return lax.dot_general(a, b, (((1,), (1,)), ((), ())), preferred_element_type=F32)


def slot_hits(routes, capacity, rows, base=0):
    top, tok_count = routes.shape
    square = (tok_count, tok_count)
    earlier = one_hot(iota(square, 0) < iota(square, 1))
    row = base + iota((rows, tok_count), 0)
    hits = [routes[k : k + 1, :] == row // capacity for k in range(top)]
    named = jnp.zeros((rows, tok_count), F32)
    for hit in hits:
        named = jnp.where(hit, 1.0, named)
    count = dot(named.astype(BF), earlier)
    here = (named > 0.0) & (count == (row % capacity).astype(F32))
    return hits, here


def dispatch_kernel(
    capacity, quarter_ref, routes_hbm, gates_hbm, grad_hbm, slots_hbm, routes_ref, gates_ref, cols_ref, slots_ref, sems
):
    chunks, rows, piece = slots_ref.shape
    start = pl.multiple_of(quarter_ref[0] * piece, piece)
    copies = [
        pltpu.make_async_copy(routes_hbm, routes_ref, sems.at[0]),
        pltpu.make_async_copy(gates_hbm, gates_ref, sems.at[1]),
        pltpu.make_async_copy(grad_hbm.at[:, pl.ds(start, piece)], cols_ref, sems.at[2]),
    ]
    for copy in copies:
        copy.start()
    for copy in copies:
        copy.wait()
    outs = []
    for c in range(chunks):
        hits, here = slot_hits(routes_ref[...], capacity, rows, c * rows)
        gate = jnp.zeros(here.shape, F32)
        for k, hit in enumerate(hits):
            gate = jnp.where(hit, gates_ref[k : k + 1, :], gate)
        weight = jnp.sum(jnp.where(here, gate, 0.0), axis=1, keepdims=True)
        slots_ref[c] = (dot(one_hot(here), cols_ref[...]) * weight).astype(BF)
        outs.append(pltpu.make_async_copy(slots_ref.at[c], slots_hbm.at[c], sems.at[3 + c]))
        outs[-1].start()
    for copy in outs:
        copy.wait()


def pick_kernel(capacity, routes_ref, pick_ref):
    tok_count, rows = pick_ref.shape
    _, here = slot_hits(routes_ref[...], capacity, rows)
    square = (tok_count, tok_count)
    pick_ref[...] = dot_t(one_hot(iota(square, 0) == iota(square, 1)), one_hot(here)).astype(BF)


def hidden_kernel(quarter_ref, rows_ref, *refs):
    downs, out_ref = refs[:-1], refs[-1]
    groups, block, piece = rows_ref.shape
    experts_here, hidden, _ = downs[0].shape
    capacity = block // experts_here
    quarters = len(downs)
    own = pl.ds(pl.multiple_of(quarter_ref[0] * piece, piece), piece)
    wide = rows_ref[...].astype(F32)
    for j in range(experts_here):
        mine = wide[:, j * capacity : (j + 1) * capacity, :]
        mine = mine.reshape(groups * capacity, piece).astype(BF)
        for d in range(quarters):
            target = lax.rem(quarter_ref[0] + quarters - d, quarters)
            value = dot_t(downs[d][j] if d else downs[0][j, :, own], mine)
            out_ref[target, j * hidden : (j + 1) * hidden, :] = value.astype(BF)


def expert_kernel(parts_ref, gate_ref, up_ref, wg_ref, wu_ref, out_hbm, out, sems):
    quarters, groups, block, piece = out.shape
    experts_here, hidden, _ = wg_ref.shape
    capacity = block // experts_here
    grads = []
    for j in range(experts_here):
        band = slice(j * hidden, (j + 1) * hidden)
        total = parts_ref[0, band, :].astype(F32)
        for c in range(1, quarters):
            total = total + parts_ref[c, band, :].astype(F32)
        d_hidden = total.T
        act = gate_ref[j].astype(F32)
        up = up_ref[j].astype(F32)
        sig = jax.nn.sigmoid(act)
        d_gate = (d_hidden * up * (sig * (1.0 + act * (1.0 - sig)))).astype(BF)
        d_up = (d_hidden * (act * sig)).astype(BF)
        grads.append((d_gate, d_up))
    copies = []
    for c in range(quarters):
        cols = slice(c * piece, (c + 1) * piece)
        values = []
        for j in range(experts_here):
            value = dot(grads[j][0], wg_ref[j, :, cols]) + dot(grads[j][1], wu_ref[j, :, cols])
            values.append(value.reshape(groups, capacity, piece))
        out[c] = jnp.concatenate(values, axis=1).astype(BF)
        copies.append(pltpu.make_async_copy(out.at[c], out_hbm.at[c], sems.at[c]))
        copies[-1].start()
    for copy in copies:
        copy.wait()


def sum_kernel(parts_ref, out_hbm, out, sems):
    chunks = max(1, out.shape[0] // 8)
    copies = []
    for n in range(out.shape[0] // chunks):
        some = slice(n * chunks, (n + 1) * chunks)
        total = parts_ref[0, some].astype(F32)
        for c in range(1, parts_ref.shape[0]):
            total = total + parts_ref[c, some].astype(F32)
        out[some] = total.astype(BF)
        copies.append(pltpu.make_async_copy(out.at[some], out_hbm.at[some], sems.at[n]))
        copies[-1].start()
    for copy in copies:
        copy.wait()


def combine_kernel(pick_ref, back_ref, out_ref):
    quarters, heads, packed, lanes = out_ref.shape
    tok_count = pick_ref.shape[0]
    part = tok_count // quarters
    tiles = packed // part
    total = dot(pick_ref[...], back_ref[...]).astype(BF)
    stacked = jnp.concatenate([total[:, n * lanes : (n + 1) * lanes] for n in range(tiles)], axis=0)
    size = quarters * packed
    to = iota((size, size), 0)
    have = iota((size, size), 1)
    token = to // packed * part + to % part
    tile = to % packed // part
    value = dot(one_hot(have == tile * tok_count + token), stacked).astype(BF)
    for c in range(quarters):
        for h in range(heads):
            out_ref[c, h] = value[c * packed : (c + 1) * packed]


def offset(index, heads):
    turned = jnp.zeros_like(index)
    step = 1
    while step < heads:
        turned = turned * 2 + index // step % 2
        step *= 2
    return turned


def finish_kernel(
    head_ref, moe_ref, near_ref, far_hbm, gain_ref, w_ref, resid_ref, grad_ref, moe, full, far_ref, sem
):
    far_copy = pltpu.make_async_copy(far_hbm, far_ref, sem.at[0])
    far_copy.start()
    quarters, heads, packed, lanes = moe_ref.shape
    part, _, width = resid_ref.shape
    tiles = packed // part
    piece = tiles * lanes
    rows = heads * PAD
    me = head_ref[0]
    row = iota((rows, heads * packed), 0)
    source = offset(row // PAD, heads) ^ me
    item = iota((rows, heads * packed), 1)
    for n in range(tiles):
        want = source * packed + n * part + row % PAD
        move = one_hot((want == item) & (row % PAD < part))
        blocks = [moe_ref[c].reshape(heads * packed, lanes) for c in range(quarters)]
        moved = dot(move, jnp.concatenate(blocks, axis=1))
        for c in range(quarters):
            start = c * piece + n * lanes
            moe[:, start : start + lanes] = moved[:, c * lanes : (c + 1) * lanes]
    count = heads // 2
    half = count * PAD
    for n, pairs_ref in enumerate((near_ref, far_ref)):
        if n:
            far_copy.wait()
        some = slice(n * half, (n + 1) * half)
        both = pairs_ref[...].astype(F32).reshape(count, 2 * part, width)
        x = both[:, :PAD].reshape(half, width)
        tail = both[:, 8:PAD].reshape(count * 8, width)
        tail = pltpu.roll(tail, count * 8 - (PAD - part), 0).reshape(count, 8, width)
        out_rows = jnp.concatenate([both[:, PAD:], tail], axis=1).reshape(half, width)
        inv_rms = lax.rsqrt(jnp.sum(x * x, axis=1, keepdims=True) / width + 1e-06)
        normed = x * inv_rms
        scaled = moe[some] * gain_ref[...]
        mean = jnp.sum(scaled * normed, axis=1, keepdims=True) / width
        value = out_rows + inv_rms * (scaled - normed * mean)
        if n == 0:
            resid_ref[...] = value[:part].reshape(part, 1, width)
        full[some] = value.astype(BF)
    product = dot_t(full[...], w_ref[...]).astype(BF)
    want = iota((heads * part, rows), 0)
    have = iota((heads * part, rows), 1)
    keep = one_hot(offset((want // part) ^ me, heads) * PAD + want % part == have)
    grad_ref[...] = dot(keep, product).astype(BF)


def call(kernel, out_shape, specs, flops, moved, scratch=(), out_specs=None, grant=GRANT):
    return pl.pallas_call(
        kernel,
        out_shape=out_shape,
        in_specs=specs,
        out_specs=out_specs or jax.tree.map(lambda _: VM, out_shape),
        scratch_shapes=scratch,
        cost_estimate=pl.CostEstimate(flops=flops, bytes_accessed=moved, transcendentals=0),
        compiler_params=pltpu.CompilerParams(vmem_limit_bytes=grant),
    )


def exchange(blocks, axis):
    return lax.all_to_all(blocks, axis, split_axis=0, concat_axis=0, tiled=True)


def shards(
    out_grad, layer_input, norm_gain, routes, gates, gate_pre, up_pre, w_gate, w_up, w_down, w_out
):
    experts_here = w_gate.shape[0]
    exp_groups = lax.axis_size("exp")
    quarters = lax.axis_size("seq")
    heads = lax.axis_size("head")
    capacity = gate_pre.shape[3]
    hidden = gate_pre.shape[4]
    tok_count, width = out_grad.shape
    piece = width // quarters
    part = tok_count // quarters
    block = experts_here * capacity
    rows = exp_groups * block
    attn = w_out.shape[0]
    packed = part * piece // LANES
    sds = jax.ShapeDtypeStruct
    quarter = lax.axis_index("seq").astype(I32).reshape(1)
    head = lax.axis_index("head").astype(I32).reshape(1)

    chunks = 4
    slots = call(
        functools.partial(dispatch_kernel, capacity),
        sds((chunks, rows // chunks, piece), BF),
        [SM, HB, HB, HB],
        2 * rows * tok_count * piece,
        1 << 20,
        [
            pltpu.VMEM(routes.T.shape, I32),
            pltpu.VMEM(gates.T.shape, F32),
            pltpu.VMEM((tok_count, piece), BF),
            pltpu.VMEM((chunks, rows // chunks, piece), BF),
            DMA((3 + chunks,)),
        ],
        HB,
        grant=None,
    )(quarter, routes.T, gates.T, out_grad)

    received = exchange(slots.reshape(exp_groups, block, piece), "exp")

    downs = [w_down]
    for d in range(1, quarters):
        start = lax.rem(quarter[0] + d, quarters) * piece
        own = lax.dynamic_slice_in_dim(w_down, start, piece, 2)
        ring = [(i, (i + d) % quarters) for i in range(quarters)]
        downs.append(lax.ppermute(own, "seq", ring))

    def own_rows(values):
        return lax.dynamic_slice_in_dim(values, quarter[0] * part, part, 0)

    def doubled(values, step):
        other = lax.ppermute(values, "head", [(i, i ^ step) for i in range(heads)])
        return jnp.concatenate([values, other], axis=0)

    own_grad = own_rows(out_grad)
    pairs = jnp.concatenate([own_rows(layer_input), own_grad[8:], own_grad[:8]], axis=0)

    partial_hidden = call(
        hidden_kernel,
        sds((quarters, experts_here * hidden, exp_groups * capacity), BF),
        [SM] + [VM] * (1 + quarters),
        2 * rows * width * hidden,
        3 << 20,
    )(quarter, received, *downs)
    summands = exchange(partial_hidden, "seq")
    parts = call(
        expert_kernel,
        sds((quarters, exp_groups, block, piece), BF),
        [VM] * 5,
        4 * rows * hidden * width,
        6 << 20,
        [pltpu.VMEM((quarters, exp_groups, block, piece), BF), DMA((quarters,))],
        HB,
    )(
        summands,
        gate_pre.reshape(experts_here, exp_groups * capacity, hidden),
        up_pre.reshape(experts_here, exp_groups * capacity, hidden),
        jnp.swapaxes(w_gate, 1, 2),
        jnp.swapaxes(w_up, 1, 2),
    )
    mine = exchange(parts, "seq")
    pairs = doubled(pairs, heads // 2)
    mine, pairs = lax.optimization_barrier((mine, pairs))
    summed = call(
        sum_kernel,
        sds((exp_groups, block, piece), BF),
        [VM],
        4 * rows * piece,
        3 << 20,
        [pltpu.VMEM((exp_groups, block, piece), BF), DMA((exp_groups // max(1, exp_groups // 8),))],
        HB,
    )(mine)
    back = exchange(summed, "exp")
    step = heads // 4
    while step > 1:
        pairs = doubled(pairs, step)
        step //= 2
    far = lax.ppermute(pairs, "head", [(i, i ^ 1) for i in range(heads)])
    late_routes, summed = lax.optimization_barrier((routes.T, summed))
    pick = call(
        functools.partial(pick_kernel, capacity),
        sds((tok_count, rows), BF),
        [VM],
        2 * rows * tok_count * tok_count,
        1 << 19,
    )(late_routes)
    back, pick, pairs, far, head = lax.optimization_barrier((back, pick, pairs, far, head))
    combined = call(
        combine_kernel,
        sds((quarters, heads, packed, LANES), BF),
        [VM] * 2,
        2 * rows * tok_count * piece,
        1 << 20,
    )(pick, back.reshape(rows, piece))
    got = exchange(combined.reshape(quarters * heads, packed, LANES), ("seq", "head"))
    resid, head_grad = call(
        finish_kernel,
        [sds((part, 1, width), F32), sds((heads * part, attn), BF)],
        [SM, VM, VM, HB, VM, VM],
        2 * heads * PAD * width * attn,
        4 << 20,
        [
            pltpu.VMEM((heads * PAD, width), F32),
            pltpu.VMEM((heads * PAD, width), BF),
            pltpu.VMEM(far.shape, BF),
            DMA((1,)),
        ],
    )(
        head,
        got.reshape(quarters, heads, packed, LANES),
        pairs,
        far,
        norm_gain[None, :],
        w_out,
    )
    return jnp.swapaxes(resid, 0, 1), head_grad[None]


def solution(mesh):
    placed = (
        P(("exp", "head"), None),
        P(("exp", "head"), None),
        P(),
        P(("exp", "head"), None),
        P(("exp", "head"), None),
        P("head", "exp", None, None, "seq"),
        P("head", "exp", None, None, "seq"),
        P("exp", None, "seq"),
        P("exp", None, "seq"),
        P("exp", "seq", None),
        P("head", None),
    )
    return jax.shard_map(
        shards,
        mesh=mesh,
        in_specs=placed,
        out_specs=(P("seq", ("exp", "head"), None), P("seq", "exp", "head")),
        check_vma=False,
    )
```
